32 devices in a mesh: groups: 2 (over y), hist: 4 (over z), head: 2 (over x), rep: 2 (over core).
Axes of the slice: x: 2, y: 2, z: 4, core: 2. Of those that a mesh axis runs over, the one named last changes fastest.
Arguments:
- item_feats: bfloat16 [4096, 4096], P(('groups', 'hist', 'rep')), parts along dimension 0, may hold values from -6 to 6
- adapter: bfloat16 [4096, 512], P('hist', 'head'), may hold values from -0.09375 to 0.09375
- hist_emb: bfloat16 [8192, 512], P(('groups', 'hist')), parts along dimension 0, may hold values from -6 to 6
- key_weight: bfloat16 [512, 512], P(None, 'head'), may hold values from -0.25 to 0.25
- value_weight: bfloat16 [512, 512], P(None, 'head'), may hold values from -0.25 to 0.25
- routes: int32 [4096, 1], P(('groups', 'hist', 'rep')), parts along dimension 0, may hold values from 0 to 3; in each aligned block of 256 rows (0 to 255, 256 to 511, ...) at most 128 rows name the same one
- cand_index: int32 [1024], P(('groups', 'hist', 'rep')), parts along dimension 0, may hold values from 0 to 255
- item_user: int32 [4096], P(('groups', 'hist', 'rep')), parts along dimension 0, may hold values from 0 to 255
- hist_user: int32 [8192], P(('groups', 'hist')), parts along dimension 0, may hold values from 0 to 255
Outputs:
- scored: bfloat16 [1024, 512], P(('groups', 'hist', 'rep'), 'head'), parts along dimension 0
The draws below stay inside these ranges and needn't reach their ends.
There are 2 independent parts, one for each index of `groups`. The reference program is written for one: setup_inputs(seed, part) draws one part's arguments, and reference() takes and returns one part's arrays. A program takes and returns all parts, laid end to end along the dimension named above; an argument that names none is the same for every part. Nothing has to cross between parts.
Inputs may be any that keep to these rules, and one draw needn't show every extreme that they name: `routes`: in the rows of one device no owner is named more than 128 times; some owner is named exactly 128 times.
All inputs are finite; a program needn't handle non-finite values.
Results may differ from the reference program's by a relative error of at most 0.0081.
Values may be sent and summed in bfloat16 or wider, within the bound.
A program may use at most 64 MiB of HBM per device.

```python
import math
import jax
import jax.numpy as jnp
import numpy as np
from jax import lax

DIN = 4096
D = 512
HEADS = 8
HS = 64
USERS = 256
ITEM_DEV = 256
HIST_DEV = 1024
CAND_DEV = 64
CAP = 128
ITEMS = 2048
HIST = 4096
CANDS = 512
N_HIST = 4
N_REP = 2


def touch_ends(drawn, key, smallest, largest):
    dims = drawn.shape
    place = [jax.random.randint(jax.random.fold_in(key, axis), (), 0, dims[axis]) for axis in range(len(dims))]
    drawn = drawn.at[tuple(place)].set(smallest)
    longest = dims.index(max(dims))
    place[longest] = (place[longest] + 1) % dims[longest]
    return drawn.at[tuple(place)].set(largest)


def block_scale(stream_key, shape, split, least, largest):
    def one(axis_at, blocks):
        steps = jax.random.uniform(jax.random.fold_in(jax.random.fold_in(stream_key, 6), axis_at), (blocks,), jnp.float32, least / len(split), largest / len(split))
        return jnp.repeat(jnp.exp(steps), shape[axis_at] // blocks).reshape((-1,) + (1,) * (len(shape) - axis_at - 1))

    factor_of = one(*split[0])
    for cut in split[1:]:
        factor_of = factor_of * one(*cut)
    return factor_of


def deal_out(stream_key, own, number, rows, amount, top, bound, lean):
    ranking = jax.random.permutation(stream_key, amount)
    crowded, usual = shares(amount, rows * top, bound, lean, True), shares(amount, rows * top, bound, lean, False)
    places = jnp.arange(amount)

    def named(lengths, rotation):
        used = int((lengths > 0).sum())
        fixed = max(1, used // 4)
        shifted = fixed + (places - fixed + rotation * (used - fixed)) % max(1, amount - fixed)
        return jnp.zeros((amount,), jnp.int32).at[ranking[jnp.where(places < fixed, places, shifted)]].set(jnp.asarray(lengths, jnp.int32))

    lengths = jnp.where(number % 4 == 0, named(crowded, number // 4), named(usual, number - number // 4 - 1))
    mixed = jax.random.permutation(jax.random.fold_in(own, 3), amount)
    giver, receiver = mixed[0:amount // 2 * 2:2], mixed[1:amount // 2 * 2:2]
    margin = jnp.minimum(lengths[giver] - 1, bound - lengths[receiver]) // 2
    margin = jnp.where((giver == ranking[0]) | (receiver == ranking[0]) | (lengths[receiver] == 0), 0, jnp.maximum(margin, 0))
    shifted = jax.random.randint(jax.random.fold_in(own, 4), (amount // 2,), 0, 1 << 20) % (margin + 1)
    lengths = lengths.at[giver].add(-shifted).at[receiver].add(shifted)
    items = jnp.searchsorted(jnp.cumsum(lengths), jnp.arange(rows * top), side="right").astype(jnp.int32)
    grid = items.reshape(top, rows).T
    grid = grid[jax.random.permutation(jax.random.fold_in(own, 1), rows)]
    rotation = jax.random.randint(jax.random.fold_in(own, 2), (rows, 1), 0, top)
    return jnp.take_along_axis(grid, (jnp.arange(top)[None, :] + rotation) % top, axis=1)


def shares(amount, total, limit, lean, full):
    portions = [(1 << 20) // math.isqrt(grade ** lean) + 1 for grade in range(1, amount + 1)]
    largest = limit if full else min(limit, max(-(-total // amount), total * portions[0] // sum(portions)))
    least = 1 if total - largest >= amount - 1 else 0
    counts, surplus = [largest] + [least] * (amount - 1), total - largest - least * (amount - 1)
    while surplus > 0:
        candidates = [i for i in range(1, amount) if counts[i] < largest] or [i for i in range(1, amount) if counts[i] < limit]
        whole, budget = sum([portions[i] for i in candidates]), surplus
        for i in candidates:
            more = min(limit - counts[i], max(1, budget * portions[i] // whole), surplus)
            counts[i] = counts[i] + more
            surplus = surplus - more
    return np.array(counts)


def centred(key, dims, scale, bound, pieces=(), kind=jnp.bfloat16):
    values = scale * jax.random.normal(key, dims, jnp.float32)
    if pieces:
        values = values * block_scale(key, dims, pieces, -0.22, 0.18)
    return jnp.clip(values, -bound, bound).astype(kind)


def setup_inputs(seed: int = 0, part: int = 0) -> dict:
    key_list = jax.random.split(jax.random.key(seed), 10)
    part_splits = jax.random.split(jax.random.fold_in(key_list[9], part), 10)
    item_feats = centred(part_splits[0], (ITEMS, DIN), 1.0, 6.0, ((0, 8),))
    adapter = centred(key_list[1], (DIN, D), DIN ** -0.5, 0.09375, ((0, 4), (1, 2)))
    hist_emb = centred(part_splits[2], (HIST, D), 1.0, 6.0, ((0, 4),))
    key_weight = centred(key_list[3], (D, D), D ** -0.5, 0.25, ((1, 2),))
    value_weight = centred(key_list[4], (D, D), D ** -0.5, 0.25, ((1, 2),))
    routes_keys = jax.random.split(jax.random.fold_in(part_splits[5], 1), ITEMS // ITEM_DEV)
    routes_turns = jax.random.permutation(jax.random.fold_in(part_splits[5], 3), ITEMS // ITEM_DEV)
    routes = jax.vmap(lambda own, number: deal_out(jax.random.fold_in(part_splits[5], 2), own, number, ITEM_DEV, N_HIST, 1, CAP, 2))(routes_keys, routes_turns).reshape((ITEMS, 1))
    cand_index = touch_ends(jax.random.randint(part_splits[6], (CANDS,), 0, ITEM_DEV), jax.random.fold_in(part_splits[6], 1), 0, ITEM_DEV - 1).astype(jnp.int32)
    item_user = touch_ends(jax.random.randint(part_splits[7], (ITEMS,), 0, USERS), jax.random.fold_in(part_splits[7], 1), 0, USERS - 1).astype(jnp.int32)
    hist_user = touch_ends(jax.random.randint(part_splits[8], (HIST,), 0, USERS), jax.random.fold_in(part_splits[8], 1), 0, USERS - 1).astype(jnp.int32)
    return {"item_feats": item_feats, "adapter": adapter, "hist_emb": hist_emb, "key_weight": key_weight, "value_weight": value_weight, "routes": routes, "cand_index": cand_index, "item_user": item_user, "hist_user": hist_user}


def reference(item_feats, adapter, hist_emb, key_weight, value_weight, routes, cand_index, item_user, hist_user):
    embedded = jnp.dot(item_feats, adapter, preferred_element_type=jnp.float32).astype(jnp.bfloat16)
    cand_rows = ((jnp.arange(CANDS, dtype=jnp.int32) // CAND_DEV) * ITEM_DEV + cand_index.astype(jnp.int32)).astype(jnp.int32)
    queries = embedded[cand_rows]
    cand_user = item_user.astype(jnp.int32)[cand_rows]
    key_rows = jnp.dot(hist_emb, key_weight, preferred_element_type=jnp.float32).astype(jnp.bfloat16)
    value_rows = jnp.dot(hist_emb, value_weight, preferred_element_type=jnp.float32).astype(jnp.bfloat16)
    owner_of = routes[:, 0].astype(jnp.int32)
    owner_hot = (owner_of.reshape(ITEMS // ITEM_DEV, ITEM_DEV)[:, :, None] == jnp.arange(N_HIST, dtype=jnp.int32)[None, None, :]).astype(jnp.int32)
    earlier = jnp.cumsum(owner_hot, axis=1) - owner_hot
    slot_of = jnp.sum(earlier * owner_hot, axis=2).reshape(ITEMS).astype(jnp.int32)
    source = jnp.arange(ITEMS, dtype=jnp.int32) // ITEM_DEV
    position = (source * CAP + slot_of).astype(jnp.int32)
    slot_total = N_HIST * N_REP * CAP
    routed = jnp.zeros((N_HIST, slot_total, D), jnp.bfloat16).at[owner_of, position].set(embedded)
    routed_user = jnp.full((N_HIST, slot_total), -1, jnp.int32).at[owner_of, position].set(item_user.astype(jnp.int32))
    set_keys = jnp.concatenate([key_rows.reshape(N_HIST, HIST_DEV, D), routed], axis=1)
    set_values = jnp.concatenate([value_rows.reshape(N_HIST, HIST_DEV, D), routed], axis=1)
    set_users = jnp.concatenate([hist_user.astype(jnp.int32).reshape(N_HIST, HIST_DEV), routed_user], axis=1)
    att_scale = float(HS) ** -0.5
    highest = lax.Precision.HIGHEST
    cand_block = math.gcd(CANDS, 512)

    def per_block(operands):
        query_block, user_block = operands
        matching = user_block[:, None, None] == set_users[None]
        counted = jnp.sum(matching.astype(jnp.float32), axis=2)
        inverse = 1.0 / jnp.maximum(counted, 1.0)

        def per_head(head_index):
            offset = (head_index * HS).astype(jnp.int32)
            query_head = lax.dynamic_slice_in_dim(query_block, offset, HS, 1).astype(jnp.float32)
            key_head = lax.dynamic_slice_in_dim(set_keys, offset, HS, 2).astype(jnp.float32)
            value_head = lax.dynamic_slice_in_dim(set_values, offset, HS, 2).astype(jnp.float32)
            scores = jnp.einsum('cd,okd->cok', query_head, key_head, precision=highest) * att_scale
            weights = lax.optimization_barrier(jax.nn.silu(scores).astype(jnp.bfloat16)).astype(jnp.float32)
            weights = jnp.where(matching, weights, 0.0)
            summed = jnp.einsum('cok,okd->cod', weights, value_head, precision=highest)
            return jnp.sum(summed * inverse[:, :, None], axis=1)

        per_heads = lax.map(per_head, jnp.arange(HEADS, dtype=jnp.int32))
        return jnp.transpose(per_heads, (1, 0, 2)).reshape(-1, D)

    blocks = lax.map(per_block, (queries.reshape(-1, cand_block, D), cand_user.reshape(-1, cand_block)))
    attended = blocks.reshape(CANDS, D)
    gating = jax.nn.silu(queries.astype(jnp.float32))
    return (gating * attended).astype(jnp.bfloat16)
```

```python
import functools

import jax
import jax.numpy as jnp
from jax import lax
from jax.experimental import pallas as pl
from jax.experimental.pallas import tpu as pltpu
from jax.sharding import PartitionSpec as P

HS = 64
USERS = 256
MESH = pl.DeviceIdType.MESH
F32 = jnp.float32
BF16 = jnp.bfloat16
NT = (((1,), (1,)), ((), ()))


def up(value, step):
    return -(-value // step) * step


def each(low, high, step):
    if high - low <= 8:
        for index in range(low, high):
            step(index)
    else:
        lax.fori_loop(low, high, lambda index, carry: (step(index), carry)[1], 0)


def iota(shape, axis):
    return lax.broadcasted_iota(jnp.int32, shape, axis)


def kernel(
    n,
    feats_hbm,
    adapter_hbm,
    hist_hbm,
    wk_hbm,
    wv_hbm,
    routes_ref,
    cand_ref,
    iuser_ref,
    huser_ref,
    out_ref,
    feats,
    ad,
    hist,
    wk,
    wv,
    k_all,
    v_all,
    acc,
    q_all,
    part_out,
    part_in,
    own_part,
    meta,
    meta_par,
    tab_all,
    ent_user,
    ent_scale,
    w_scr,
    local,
    feat_sem,
    z_send,
    z_recv,
    y_send,
    y_recv,
    p_send,
    p_recv,
    pp_send,
    pp_recv,
    q_send,
    q_recv,
    o_send,
    o_recv,
    t_send,
    t_recv,
    pair_send,
    pair_recv,
):
    me = lax.axis_index("hist")
    g = lax.axis_index("groups")
    r = lax.axis_index("rep")
    og, orep = 1 - g, 1 - r
    sign = jnp.where(me < n // 2, 1, -1)

    def peer(d):
        return lax.rem(me + sign * d + n, n)

    items, block = feats.shape[1], feats.shape[2]
    cols = ad.shape[2]
    heads = cols // HS
    cands = q_all.shape[1]
    events = hist.shape[0]
    entries = k_all.shape[0]
    owners = up(n, 8)
    rows = block // 4

    def share(a, b):
        return pl.ds(pl.multiple_of((a * 2 + b) * rows, rows), rows)

    def remote(src, dst, send, recv, where):
        return pltpu.make_async_remote_copy(
            src_ref=src, dst_ref=dst, send_sem=send, recv_sem=recv, device_id=where, device_id_type=MESH
        )

    barrier = pltpu.get_barrier_semaphore()
    each(1, n, lambda d: pl.semaphore_signal(barrier, inc=1, device_id={"hist": peer(d)}, device_id_type=MESH))
    pl.semaphore_signal(barrier, inc=1, device_id={"rep": orep}, device_id_type=MESH)
    pl.semaphore_signal(barrier, inc=1, device_id={"groups": og}, device_id_type=MESH)

    own_ad = pltpu.make_async_copy(adapter_hbm, ad.at[me], local.at[0])
    own_hist = pltpu.make_async_copy(hist_hbm, hist, local.at[1])
    own_wk = pltpu.make_async_copy(wk_hbm, wk, local.at[2])
    own_wv = pltpu.make_async_copy(wv_hbm, wv, local.at[3])
    for copy in (own_hist, own_wk, own_wv, own_ad):
        copy.start()

    def feat_copy(s):
        return pltpu.make_async_copy(
            feats_hbm.at[:, pl.ds(pl.multiple_of(s * block, 128), block)], feats.at[s], feat_sem.at[s]
        )

    each(0, n, lambda s: feat_copy(s).start())
    pl.semaphore_wait(barrier, n + 1)

    def z_copy(to):
        return remote(
            adapter_hbm.at[share(g, r)], ad.at[me, share(g, r)], z_send.at[to], z_recv.at[me], {"hist": to}
        )

    each(1, n, lambda d: z_copy(peer(n - d)).start())

    route_row = routes_ref[...].astype(F32)
    user_row = iuser_ref[...].astype(F32)

    def hot(row, count):
        shape = (count, row.shape[1])
        return jnp.where(iota(shape, 0).astype(F32) == row, 1.0, 0.0)

    owner_hot = hot(route_row, owners)
    user_hot = hot(user_row, USERS).astype(BF16)
    counts = lax.dot_general(owner_hot.astype(BF16), user_hot, NT, preferred_element_type=F32)
    meta[0:owners, 0:USERS] = counts
    meta[owners : owners + 1, 0:items] = user_row
    meta[owners + 1 : owners + 2, 0:items] = route_row
    meta_copy = remote(meta, meta_par, pair_send.at[0], pair_recv.at[0], {"rep": orep})
    meta_copy.start()

    cand_hot_t = hot(cand_ref[...].astype(F32), items)
    cand_hot = cand_hot_t.T.astype(BF16)
    cand_user = jnp.dot(
        jnp.broadcast_to(user_row, (8, items)).astype(BF16), cand_hot_t.astype(BF16), preferred_element_type=F32
    )
    event_row = huser_ref[...].astype(F32)
    event_hot = hot(event_row, USERS).astype(BF16)
    mine = jnp.where(iota((owners, events), 0) == me, 1.0, 0.0)
    event_counts = lax.dot_general(mine.astype(BF16), event_hot, NT, preferred_element_type=F32)

    meta_copy.wait_recv()
    tab_all[me, 0:owners, 0:USERS] = counts + event_counts + meta_par[0:owners, 0:USERS]
    tab_all[me, owners : owners + 8, 0:cands] = cand_user

    def t_copy(to):
        return remote(tab_all.at[me], tab_all.at[me], t_send.at[to], t_recv.at[me], {"hist": to})

    each(1, n, lambda d: t_copy(peer(d)).start())

    own_hist.wait()
    own_wk.wait()
    own_wv.wait()
    step_rows = min(events, 512)
    for start in range(0, events, step_rows):
        part = hist[start : start + step_rows, :]
        k_all[start : start + step_rows, :] = jnp.dot(part, wk[...], preferred_element_type=F32).astype(BF16)
        v_all[start : start + step_rows, :] = jnp.dot(part, wv[...], preferred_element_type=F32).astype(BF16)

    each(0, n, lambda s: feat_copy(s).wait())
    own_ad.wait()
    acc[...] = jnp.dot(feats[me], ad[me], preferred_element_type=F32)

    def hop(src, a, b, sends, recvs, where):
        ref = ad.at[src, share(a, b)]
        return remote(ref, ref, sends.at[src], recvs.at[src], where)

    def first(d):
        src = peer(d)
        hop(src, g, r, z_send, z_recv, {"hist": src}).wait_recv()
        hop(src, g, r, y_send, y_recv, {"groups": og}).start()
        hop(src, g, r, p_send, p_recv, {"rep": orep}).start()

    each(1, n, first)

    each(1, n, lambda d: remote(
        tab_all.at[peer(d)], tab_all.at[peer(d)], t_send.at[peer(d)], t_recv.at[peer(d)], {"hist": peer(d)}
    ).wait_recv())
    table = lax.fori_loop(
        0, n, lambda s, t: t + tab_all[s, 0:owners, 0:USERS], jnp.zeros((owners, USERS), F32)
    )
    high = jnp.floor(table * (1.0 / 256.0))
    split = jnp.concatenate([high, table - 256.0 * high], axis=0).astype(BF16)

    def scale_of(users_hot, owners_hot):
        both = jnp.dot(split, users_hot, preferred_element_type=F32)
        found = 256.0 * both[0:owners] + both[owners:]
        return 1.0 / jnp.maximum(jnp.sum(found * owners_hot, axis=0, keepdims=True), 1.0)

    par_user = meta_par[owners : owners + 1, 0:items]
    par_route = meta_par[owners + 1 : owners + 2, 0:items]
    ent_user[:, 0:events] = jnp.broadcast_to(event_row, (8, events))
    ent_user[:, events : events + items] = jnp.broadcast_to(user_row, (8, items))
    ent_user[:, events + items :] = jnp.broadcast_to(par_user, (8, items))
    ent_scale[:, 0:events] = jnp.broadcast_to(scale_of(event_hot, mine), (8, events))
    ent_scale[:, events : events + items] = jnp.broadcast_to(scale_of(user_hot, owner_hot), (8, items))
    ent_scale[:, events + items :] = jnp.broadcast_to(
        scale_of(hot(par_user, USERS).astype(BF16), hot(par_route, owners)), (8, items)
    )

    def second(d):
        src = peer(d)
        hop(src, og, r, y_send, y_recv, {"groups": og}).wait_recv()
        hop(src, og, r, pp_send, pp_recv, {"rep": orep}).start()

    each(1, n, second)

    def third(d):
        src = peer(d)
        hop(src, g, orep, p_send, p_recv, {"rep": orep}).wait_recv()
        hop(src, og, orep, pp_send, pp_recv, {"rep": orep}).wait_recv()
        acc[...] += jnp.dot(feats[src], ad[src], preferred_element_type=F32)

    each(1, n, third)

    embedded = acc[...].astype(BF16)
    own_q = jnp.dot(cand_hot, embedded, preferred_element_type=F32)
    q_all[me] = own_q.astype(BF16)

    def q_copy(to):
        return remote(q_all.at[me], q_all.at[me], q_send.at[to], q_recv.at[me], {"hist": to})

    each(1, n, lambda d: q_copy(peer(n - d)).start())
    k_all[events : events + items, :] = embedded
    v_all[events : events + items, :] = embedded
    emb_copy = remote(
        k_all.at[pl.ds(events, items)],
        k_all.at[pl.ds(events + items, items)],
        pair_send.at[1],
        pair_recv.at[1],
        {"rep": orep},
    )
    emb_copy.start()

    head_of = iota((1, cols), 1) // HS
    eye = iota((cands, cands), 0) == iota((cands, cands), 1)
    width = math_block(entries)

    def user_column(p):
        row = tab_all[p, owners : owners + 1, 0:cands]
        return jnp.sum(jnp.where(eye, row, 0.0), axis=1, keepdims=True)

    def q_wait(p):
        remote(q_all.at[p], q_all.at[p], q_send.at[p], q_recv.at[p], {"hist": p}).wait_recv()

    def o_copy(to):
        return remote(part_out.at[to], part_in.at[me], o_send.at[to], o_recv.at[me], {"hist": to})

    def chunk(pa, pb, opening):
        if not opening:
            q_wait(pa)
        q_wait(pb)
        q = jnp.concatenate([q_all[pa], q_all[pb]], axis=0) * jnp.asarray(0.5 * HS**-0.5, BF16)
        ucol = jnp.concatenate([user_column(pa), user_column(pb)], axis=0)
        count = 2 * cands
        stacked = jnp.concatenate([jnp.where(head_of == h, q, jnp.zeros_like(q)) for h in range(heads)], axis=0)
        for start in range(0, entries, width):
            if opening and start + width > events + items and start <= events + items:
                emb_copy.wait_recv()
                v_all[events + items :, :] = k_all[events + items :, :]
            half = lax.dot_general(stacked, k_all[start : start + width, :], NT, preferred_element_type=F32)
            scale = jnp.where(
                ucol == ent_user[0:1, start : start + width], ent_scale[0:1, start : start + width], 0.0
            )
            weight = (half + half * jnp.tanh(half)).reshape(heads, count, width) * scale[None]
            w_scr[:, start : start + width] = weight.reshape(heads * count, width).astype(BF16)
        mixed = jnp.dot(w_scr[...], v_all[...], preferred_element_type=F32)
        total = mixed[0:count]
        for h in range(1, heads):
            total = jnp.where(head_of == h, mixed[h * count : (h + 1) * count], total)
        if opening:
            own_part[...] = total[0:cands]
        else:
            part_out[pa] = total[0:cands].astype(BF16)
            o_copy(pa).start()
        part_out[pb] = total[cands:].astype(BF16)
        o_copy(pb).start()

    chunk(me, peer(1), True)
    each(1, n // 2, lambda c: chunk(peer(2 * c), peer(2 * c + 1), False))

    def collect(d):
        src = peer(d)
        remote(part_out.at[src], part_in.at[src], o_send.at[src], o_recv.at[src], {"hist": src}).wait_recv()
        own_part[...] += part_in[src].astype(F32)

    each(1, n, collect)
    gate = own_q * (0.5 + 0.5 * jnp.tanh(0.5 * own_q))
    out_ref[...] = (gate * own_part[...]).astype(BF16)

    def drain(d):
        p = peer(d)
        z_copy(p).wait_send()
        hop(p, g, r, y_send, y_recv, {"groups": og}).wait_send()
        hop(p, g, r, p_send, p_recv, {"rep": orep}).wait_send()
        hop(p, og, r, pp_send, pp_recv, {"rep": orep}).wait_send()
        t_copy(p).wait_send()
        q_copy(p).wait_send()
        o_copy(p).wait_send()

    each(1, n, drain)
    meta_copy.wait_send()
    emb_copy.wait_send()


def math_block(entries):
    return 256 if entries % 256 == 0 else 128


def body(item_feats, adapter, hist_emb, key_weight, value_weight, routes, cand_index, item_user, hist_user):
    n = lax.axis_size("hist")
    items, depth = item_feats.shape
    block, cols = adapter.shape
    events, dim = hist_emb.shape
    cands = cand_index.shape[0]
    heads = cols // HS
    owners = up(n, 8)
    wide = up(max(USERS, items, cands), 128)
    entries = events + 2 * items
    anywhere = pl.BlockSpec(memory_space=pl.ANY)
    vmem = pl.BlockSpec(memory_space=pltpu.VMEM)
    dma = pltpu.SemaphoreType.DMA
    return pl.pallas_call(
        functools.partial(kernel, n),
        out_shape=jax.ShapeDtypeStruct((cands, cols), BF16),
        in_specs=[anywhere] * 5 + [vmem] * 4,
        out_specs=vmem,
        scratch_shapes=[
            pltpu.VMEM((n, items, block), BF16),
            pltpu.VMEM((n, block, cols), BF16),
            pltpu.VMEM((events, dim), BF16),
            pltpu.VMEM((dim, cols), BF16),
            pltpu.VMEM((dim, cols), BF16),
            pltpu.VMEM((entries, cols), BF16),
            pltpu.VMEM((entries, cols), BF16),
            pltpu.VMEM((items, cols), F32),
            pltpu.VMEM((n, cands, cols), BF16),
            pltpu.VMEM((n, cands, cols), BF16),
            pltpu.VMEM((n, cands, cols), BF16),
            pltpu.VMEM((cands, cols), F32),
            pltpu.VMEM((owners + 8, wide), F32),
            pltpu.VMEM((owners + 8, wide), F32),
            pltpu.VMEM((n, owners + 8, wide), F32),
            pltpu.VMEM((8, entries), F32),
            pltpu.VMEM((8, entries), F32),
            pltpu.VMEM((heads * 2 * cands, entries), BF16),
            dma((4,)),
            dma((n,)),
        ]
        + [dma((n,))] * 14
        + [dma((2,)), dma((2,))],
        compiler_params=pltpu.CompilerParams(
            collective_id=0, has_side_effects=True, vmem_limit_bytes=48 * 1024 * 1024
        ),
    )(
        item_feats,
        adapter,
        hist_emb,
        key_weight,
        value_weight,
        routes.reshape(1, items),
        cand_index.reshape(1, cands),
        item_user.reshape(1, items),
        hist_user.reshape(1, events),
    )


def solution(mesh):
    placed = (
        P(("groups", "hist", "rep"), None),
        P("hist", "head"),
        P(("groups", "hist"), None),
        P(None, "head"),
        P(None, "head"),
        P(("groups", "hist", "rep"), None),
        P(("groups", "hist", "rep")),
        P(("groups", "hist", "rep")),
        P(("groups", "hist")),
    )
    return jax.shard_map(
        body,
        mesh=mesh,
        in_specs=placed,
        out_specs=P(("groups", "hist", "rep"), "head"),
        check_vma=False,
    )
```

```python
import functools

import jax
import jax.numpy as jnp
from jax import lax
from jax.experimental import pallas as pl
from jax.experimental.pallas import tpu as pltpu
from jax.sharding import PartitionSpec as P

HS = 64
SUB = 2
USERS = 256
MESH = pl.DeviceIdType.MESH
F32 = jnp.float32
BF16 = jnp.bfloat16
NT = (((1,), (1,)), ((), ()))


def up(value, step):
    return -(-value // step) * step


def each(low, high, step):
    if high - low <= 8:
        for index in range(low, high):
            step(index)
    else:
        lax.fori_loop(low, high, lambda index, carry: (step(index), carry)[1], 0)


def iota(shape, axis):
    return lax.broadcasted_iota(jnp.int32, shape, axis)


def kernel(
    n,
    feats_hbm,
    adapter_hbm,
    hist_hbm,
    wk_hbm,
    wv_hbm,
    routes_hbm,
    cand_hbm,
    iuser_hbm,
    huser_hbm,
    out_ref,
    routes_ref,
    cand_ref,
    iuser_ref,
    huser_ref,
    feats,
    ad,
    hist,
    wk,
    wv,
    k_all,
    v_all,
    acc,
    q_all,
    part_out,
    part_in,
    own_part,
    meta,
    meta_par,
    tab_all,
    ent_user,
    ent_scale,
    w_scr,
    local,
    feat_sem,
    left_send,
    right_send,
    z_recv,
    y_send,
    y_recv,
    p_send,
    p_recv,
    pp_send,
    pp_recv,
    q_send,
    q_recv,
    o_send,
    o_recv,
    t_send,
    t_recv,
    pair_send,
    pair_recv,
):
    me = lax.axis_index("hist")
    g = lax.axis_index("groups")
    r = lax.axis_index("rep")
    og, orep = 1 - g, 1 - r
    sign = jnp.where(me < n // 2, 1, -1)

    def peer(d):
        return lax.rem(me + sign * d + n, n)

    items, block = feats.shape[1], feats.shape[2]
    cols = ad.shape[2]
    heads = cols // HS
    cands = q_all.shape[1]
    events = hist.shape[0]
    entries = k_all.shape[0]
    owners = up(n, 8)
    rows = block // (4 * SUB)

    def share(a, b, k):
        return pl.ds(pl.multiple_of(((a * 2 + b) * SUB + k) * rows, rows), rows)

    def remote(src, dst, send, recv, where):
        return pltpu.make_async_remote_copy(
            src_ref=src, dst_ref=dst, send_sem=send, recv_sem=recv, device_id=where, device_id_type=MESH
        )

    barrier = pltpu.get_barrier_semaphore()
    each(1, n, lambda d: pl.semaphore_signal(barrier, inc=1, device_id={"hist": peer(d)}, device_id_type=MESH))
    pl.semaphore_signal(barrier, inc=1, device_id={"rep": orep}, device_id_type=MESH)
    pl.semaphore_signal(barrier, inc=1, device_id={"groups": og}, device_id_type=MESH)

    own_ad = pltpu.make_async_copy(adapter_hbm, ad.at[me], local.at[0])
    own_hist = pltpu.make_async_copy(hist_hbm, hist, local.at[1])
    own_wk = pltpu.make_async_copy(wk_hbm, wk, local.at[2])
    own_wv = pltpu.make_async_copy(wv_hbm, wv, local.at[3])
    small = [
        pltpu.make_async_copy(source, target, local.at[4 + place])
        for place, (source, target) in enumerate(
            ((routes_hbm, routes_ref), (iuser_hbm, iuser_ref), (cand_hbm, cand_ref), (huser_hbm, huser_ref))
        )
    ]
    for copy in (*small, own_hist, own_wk, own_wv, own_ad):
        copy.start()

    def feat_copy(s):
        return pltpu.make_async_copy(
            feats_hbm.at[:, pl.ds(pl.multiple_of(s * block, 128), block)], feats.at[s], feat_sem.at[s]
        )

    each(0, n, lambda s: feat_copy(s).start())
    pl.semaphore_wait(barrier, n + 1)

    def to_right(src, k, ref):
        return remote(
            ref, ad.at[src, share(g, r, k)], right_send.at[src * SUB + k], z_recv.at[src * SUB + k], {"hist": me + 1}
        )

    def to_left(src, k, ref):
        return remote(
            ref, ad.at[src, share(g, r, k)], left_send.at[src * SUB + k], z_recv.at[src * SUB + k], {"hist": me - 1}
        )

    def piece(src, a, b, k):
        return ad.at[src, share(a, b, k)]

    for k in range(SUB):

        @pl.when(me < n - 1)
        def _():
            to_right(me, k, adapter_hbm.at[share(g, r, k)]).start()

        @pl.when(me > 0)
        def _():
            to_left(me, k, adapter_hbm.at[share(g, r, k)]).start()

    for copy in small:
        copy.wait()
    route_row = routes_ref[...].astype(F32)
    user_row = iuser_ref[...].astype(F32)

    def hot(row, count):
        shape = (count, row.shape[1])
        return jnp.where(iota(shape, 0).astype(F32) == row, 1.0, 0.0)

    owner_hot = hot(route_row, owners)
    user_hot = hot(user_row, USERS).astype(BF16)
    counts = lax.dot_general(owner_hot.astype(BF16), user_hot, NT, preferred_element_type=F32)
    meta[0:owners, 0:USERS] = counts
    meta[owners : owners + 1, 0:items] = user_row
    meta[owners + 1 : owners + 2, 0:items] = route_row
    meta_copy = remote(meta, meta_par, pair_send.at[0], pair_recv.at[0], {"rep": orep})
    meta_copy.start()

    cand_hot_t = hot(cand_ref[...].astype(F32), items)
    cand_hot = cand_hot_t.T.astype(BF16)
    cand_user = jnp.dot(
        jnp.broadcast_to(user_row, (8, items)).astype(BF16), cand_hot_t.astype(BF16), preferred_element_type=F32
    )
    event_row = huser_ref[...].astype(F32)
    event_hot = hot(event_row, USERS).astype(BF16)
    mine = jnp.where(iota((owners, events), 0) == me, 1.0, 0.0)
    event_counts = lax.dot_general(mine.astype(BF16), event_hot, NT, preferred_element_type=F32)

    meta_copy.wait_recv()
    tab_all[me, 0:owners, 0:USERS] = counts + event_counts + meta_par[0:owners, 0:USERS]
    tab_all[me, owners : owners + 8, 0:cands] = cand_user

    def t_copy(to):
        return remote(tab_all.at[me], tab_all.at[me], t_send.at[to], t_recv.at[me], {"hist": to})

    each(1, n, lambda d: t_copy(peer(d)).start())

    def hop(src, a, b, k, sends, recvs, where):
        ref = piece(src, a, b, k)
        return remote(ref, ref, sends.at[src * SUB + k], recvs.at[src * SUB + k], where)

    def spread(src, k):
        hop(src, g, r, k, y_send, y_recv, {"groups": og}).start()
        hop(src, g, r, k, p_send, p_recv, {"rep": orep}).start()

    def z_arrive(s):
        for k in range(SUB):

            @pl.when(me >= s)
            def _():
                src = me - s
                ref = piece(src, g, r, k)
                to_right(src, k, ref).wait_recv()

                @pl.when(me < n - 1)
                def _():
                    to_right(src, k, ref).start()

                spread(src, k)

            @pl.when(me + s < n)
            def _():
                src = me + s
                ref = piece(src, g, r, k)
                to_left(src, k, ref).wait_recv()

                @pl.when(me > 0)
                def _():
                    to_left(src, k, ref).start()

                spread(src, k)

    def y_pass(src):
        for k in range(SUB):
            hop(src, og, r, k, y_send, y_recv, {"groups": og}).wait_recv()
            hop(src, og, r, k, pp_send, pp_recv, {"rep": orep}).start()

    def y_arrive(s):
        @pl.when(me >= s)
        def _():
            y_pass(me - s)

        @pl.when(me + s < n)
        def _():
            y_pass(me + s)

    def project():
        own_hist.wait()
        own_wk.wait()
        own_wv.wait()
        step_rows = min(events, 512)
        for start in range(0, events, step_rows):
            part = hist[start : start + step_rows, :]
            k_all[start : start + step_rows, :] = jnp.dot(part, wk[...], preferred_element_type=F32).astype(BF16)
            v_all[start : start + step_rows, :] = jnp.dot(part, wv[...], preferred_element_type=F32).astype(BF16)

    def own_block():
        each(0, n, lambda s: feat_copy(s).wait())
        own_ad.wait()
        acc[...] = jnp.dot(feats[me], ad[me], preferred_element_type=F32)

    z_arrive(1)
    project()
    z_arrive(2)
    y_arrive(1)
    own_block()
    each(3, n, lambda s: (z_arrive(s), y_arrive(s - 1)))

    each(1, n, lambda d: remote(
        tab_all.at[peer(d)], tab_all.at[peer(d)], t_send.at[peer(d)], t_recv.at[peer(d)], {"hist": peer(d)}
    ).wait_recv())
    table = lax.fori_loop(
        0, n, lambda s, t: t + tab_all[s, 0:owners, 0:USERS], jnp.zeros((owners, USERS), F32)
    )
    high = jnp.floor(table * (1.0 / 256.0))
    split = jnp.concatenate([high, table - 256.0 * high], axis=0).astype(BF16)

    def scale_of(users_hot, owners_hot):
        both = jnp.dot(split, users_hot, preferred_element_type=F32)
        found = 256.0 * both[0:owners] + both[owners:]
        return 1.0 / jnp.maximum(jnp.sum(found * owners_hot, axis=0, keepdims=True), 1.0)

    par_user = meta_par[owners : owners + 1, 0:items]
    par_route = meta_par[owners + 1 : owners + 2, 0:items]
    ent_user[:, 0:events] = jnp.broadcast_to(event_row, (8, events))
    ent_user[:, events : events + items] = jnp.broadcast_to(user_row, (8, items))
    ent_user[:, events + items :] = jnp.broadcast_to(par_user, (8, items))
    ent_scale[:, 0:events] = jnp.broadcast_to(scale_of(event_hot, mine), (8, events))
    ent_scale[:, events : events + items] = jnp.broadcast_to(scale_of(user_hot, owner_hot), (8, items))
    ent_scale[:, events + items :] = jnp.broadcast_to(
        scale_of(hot(par_user, USERS).astype(BF16), hot(par_route, owners)), (8, items)
    )

    y_arrive(n - 1)

    def third(d):
        src = peer(d)
        for k in range(SUB):
            hop(src, g, orep, k, p_send, p_recv, {"rep": orep}).wait_recv()
            hop(src, og, orep, k, pp_send, pp_recv, {"rep": orep}).wait_recv()
        acc[...] += jnp.dot(feats[src], ad[src], preferred_element_type=F32)

    each(1, n, third)

    embedded = acc[...].astype(BF16)
    own_q = jnp.dot(cand_hot, embedded, preferred_element_type=F32)
    q_all[me] = own_q.astype(BF16)

    def q_copy(to):
        return remote(q_all.at[me], q_all.at[me], q_send.at[to], q_recv.at[me], {"hist": to})

    each(1, n, lambda d: q_copy(peer(n - d)).start())
    k_all[events : events + items, :] = embedded
    v_all[events : events + items, :] = embedded
    emb_copy = remote(
        k_all.at[pl.ds(events, items)],
        k_all.at[pl.ds(events + items, items)],
        pair_send.at[1],
        pair_recv.at[1],
        {"rep": orep},
    )
    emb_copy.start()

    head_of = iota((1, cols), 1) // HS
    eye = iota((cands, cands), 0) == iota((cands, cands), 1)
    width = math_block(entries)

    def user_column(p):
        row = tab_all[p, owners : owners + 1, 0:cands]
        return jnp.sum(jnp.where(eye, row, 0.0), axis=1, keepdims=True)

    def q_wait(p):
        remote(q_all.at[p], q_all.at[p], q_send.at[p], q_recv.at[p], {"hist": p}).wait_recv()

    def o_copy(to):
        return remote(part_out.at[to], part_in.at[me], o_send.at[to], o_recv.at[me], {"hist": to})

    def chunk(pa, pb, opening):
        if not opening:
            q_wait(pa)
        q_wait(pb)
        q = jnp.concatenate([q_all[pa], q_all[pb]], axis=0) * jnp.asarray(0.5 * HS**-0.5, BF16)
        ucol = jnp.concatenate([user_column(pa), user_column(pb)], axis=0)
        count = 2 * cands
        stacked = jnp.concatenate([jnp.where(head_of == h, q, jnp.zeros_like(q)) for h in range(heads)], axis=0)
        for start in range(0, entries, width):
            if opening and start + width > events + items and start <= events + items:
                emb_copy.wait_recv()
                v_all[events + items :, :] = k_all[events + items :, :]
            half = lax.dot_general(stacked, k_all[start : start + width, :], NT, preferred_element_type=F32)
            scale = jnp.where(
                ucol == ent_user[0:1, start : start + width], ent_scale[0:1, start : start + width], 0.0
            )
            weight = (half + half * jnp.tanh(half)).reshape(heads, count, width) * scale[None]
            w_scr[:, start : start + width] = weight.reshape(heads * count, width).astype(BF16)
        mixed = jnp.dot(w_scr[...], v_all[...], preferred_element_type=F32)
        total = mixed[0:count]
        for h in range(1, heads):
            total = jnp.where(head_of == h, mixed[h * count : (h + 1) * count], total)
        if opening:
            own_part[...] = total[0:cands]
        else:
            part_out[pa] = total[0:cands].astype(BF16)
            o_copy(pa).start()
        part_out[pb] = total[cands:].astype(BF16)
        o_copy(pb).start()

    chunk(me, peer(1), True)
    each(1, n // 2, lambda c: chunk(peer(2 * c), peer(2 * c + 1), False))

    def collect(d):
        src = peer(d)
        remote(part_out.at[src], part_in.at[src], o_send.at[src], o_recv.at[src], {"hist": src}).wait_recv()
        own_part[...] += part_in[src].astype(F32)

    each(1, n, collect)
    gate = own_q * (0.5 + 0.5 * jnp.tanh(0.5 * own_q))
    out_ref[...] = (gate * own_part[...]).astype(BF16)

    def drain(d):
        p = peer(d)
        for k in range(SUB):
            hop(p, g, r, k, y_send, y_recv, {"groups": og}).wait_send()
            hop(p, g, r, k, p_send, p_recv, {"rep": orep}).wait_send()
            hop(p, og, r, k, pp_send, pp_recv, {"rep": orep}).wait_send()
        t_copy(p).wait_send()
        q_copy(p).wait_send()
        o_copy(p).wait_send()

    each(1, n, drain)

    def drain_right(s):
        @pl.when((me >= s) & (me < n - 1))
        def _():
            for k in range(SUB):
                to_right(me - s, k, piece(me - s, g, r, k)).wait_send()

    def drain_left(s):
        @pl.when((me + s < n) & (me > 0))
        def _():
            for k in range(SUB):
                to_left(me + s, k, piece(me + s, g, r, k)).wait_send()

    each(0, n, lambda s: (drain_right(s), drain_left(s)))
    meta_copy.wait_send()
    emb_copy.wait_send()


def math_block(entries):
    return 256 if entries % 256 == 0 else 128


def body(item_feats, adapter, hist_emb, key_weight, value_weight, routes, cand_index, item_user, hist_user):
    n = lax.axis_size("hist")
    items, depth = item_feats.shape
    block, cols = adapter.shape
    events, dim = hist_emb.shape
    cands = cand_index.shape[0]
    heads = cols // HS
    owners = up(n, 8)
    wide = up(max(USERS, items, cands), 128)
    entries = events + 2 * items
    hbm = pl.BlockSpec(memory_space=pltpu.HBM)
    vmem = pl.BlockSpec(memory_space=pltpu.VMEM)
    dma = pltpu.SemaphoreType.DMA
    return pl.pallas_call(
        functools.partial(kernel, n),
        out_shape=jax.ShapeDtypeStruct((cands, cols), BF16),
        in_specs=[hbm] * 9,
        out_specs=vmem,
        scratch_shapes=[
            pltpu.VMEM((1, items), jnp.int32),
            pltpu.VMEM((1, cands), jnp.int32),
            pltpu.VMEM((1, items), jnp.int32),
            pltpu.VMEM((1, events), jnp.int32),
            pltpu.VMEM((n, items, block), BF16),
            pltpu.VMEM((n, block, cols), BF16),
            pltpu.VMEM((events, dim), BF16),
            pltpu.VMEM((dim, cols), BF16),
            pltpu.VMEM((dim, cols), BF16),
            pltpu.VMEM((entries, cols), BF16),
            pltpu.VMEM((entries, cols), BF16),
            pltpu.VMEM((items, cols), F32),
            pltpu.VMEM((n, cands, cols), BF16),
            pltpu.VMEM((n, cands, cols), BF16),
            pltpu.VMEM((n, cands, cols), BF16),
            pltpu.VMEM((cands, cols), F32),
            pltpu.VMEM((owners + 8, wide), F32),
            pltpu.VMEM((owners + 8, wide), F32),
            pltpu.VMEM((n, owners + 8, wide), F32),
            pltpu.VMEM((8, entries), F32),
            pltpu.VMEM((8, entries), F32),
            pltpu.VMEM((heads * 2 * cands, entries), BF16),
            dma((8,)),
            dma((n,)),
        ]
        + [dma((n * SUB,))] * 9
        + [dma((n,))] * 6
        + [dma((2,)), dma((2,))],
        compiler_params=pltpu.CompilerParams(
            collective_id=0, has_side_effects=True
        ),
    )(
        item_feats,
        adapter,
        hist_emb,
        key_weight,
        value_weight,
        routes.reshape(1, items),
        cand_index.reshape(1, cands),
        item_user.reshape(1, items),
        hist_user.reshape(1, events),
    )


def solution(mesh):
    placed = (
        P(("groups", "hist", "rep"), None),
        P("hist", "head"),
        P(("groups", "hist"), None),
        P(None, "head"),
        P(None, "head"),
        P(("groups", "hist", "rep"), None),
        P(("groups", "hist", "rep")),
        P(("groups", "hist", "rep")),
        P(("groups", "hist")),
    )
    return jax.shard_map(
        body,
        mesh=mesh,
        in_specs=placed,
        out_specs=P(("groups", "hist", "rep"), "head"),
        check_vma=False,
    )
```

```python
import functools

import jax
import jax.numpy as jnp
from jax import lax
from jax.experimental import pallas as pl
from jax.experimental.pallas import tpu as pltpu
from jax.sharding import PartitionSpec as P

HS = 64
USERS = 256
MESH = pl.DeviceIdType.MESH
F32 = jnp.float32
BF16 = jnp.bfloat16
NT = (((1,), (1,)), ((), ()))


def up(value, step):
    return -(-value // step) * step


def each(low, high, step):
    if high - low <= 8:
        for index in range(low, high):
            step(index)
    else:
        lax.fori_loop(low, high, lambda index, carry: (step(index), carry)[1], 0)


def pieces(block):
    return max(1, min(4, block // 64))


def iota(shape, axis):
    return lax.broadcasted_iota(jnp.int32, shape, axis)


def kernel(
    n,
    feats_hbm,
    adapter_hbm,
    hist_hbm,
    wk_hbm,
    wv_hbm,
    routes_hbm,
    cand_hbm,
    iuser_hbm,
    huser_hbm,
    out_ref,
    routes_ref,
    cand_ref,
    iuser_ref,
    huser_ref,
    feats,
    ad,
    hist,
    wk,
    wv,
    k_all,
    v_all,
    acc,
    q_all,
    part_out,
    part_in,
    own_part,
    meta,
    meta_par,
    tab_all,
    ent_user,
    ent_scale,
    w_scr,
    local,
    feat_sem,
    left_send,
    right_send,
    z_recv,
    y_send,
    y_recv,
    p_send,
    p_recv,
    pp_send,
    pp_recv,
    q_send,
    q_recv,
    o_send,
    o_recv,
    t_send,
    t_recv,
    pair_send,
    pair_recv,
):
    me = lax.axis_index("hist")
    g = lax.axis_index("groups")
    r = lax.axis_index("rep")
    og, orep = 1 - g, 1 - r
    sign = jnp.where(me < n // 2, 1, -1)

    def peer(d):
        if n > 8:
            return lax.rem(me + sign * d + n, n)
        found = 0
        for at in range(n):
            nearest = sorted(range(n), key=lambda p: abs(p - at))
            found = jnp.where(me == at, nearest[d], found)
        return found

    items, block = feats.shape[1], feats.shape[2]
    cols = ad.shape[2]
    heads = cols // HS
    cands = q_all.shape[1]
    events = hist.shape[0]
    entries = k_all.shape[0]
    owners = up(n, 8)
    sub = pieces(block)
    rows = block // (4 * sub)

    def share(a, b, k):
        return pl.ds(pl.multiple_of(((a * 2 + b) * sub + k) * rows, rows), rows)

    def remote(src, dst, send, recv, where):
        return pltpu.make_async_remote_copy(
            src_ref=src, dst_ref=dst, send_sem=send, recv_sem=recv, device_id=where, device_id_type=MESH
        )

    barrier = pltpu.get_barrier_semaphore()
    has_left, has_right = me > 0, me < n - 1

    @pl.when(has_right)
    def _():
        pl.semaphore_signal(barrier, inc=1, device_id={"hist": me + 1}, device_id_type=MESH)

    @pl.when(has_left)
    def _():
        pl.semaphore_signal(barrier, inc=1, device_id={"hist": me - 1}, device_id_type=MESH)

    pl.semaphore_signal(barrier, inc=1, device_id={"rep": orep}, device_id_type=MESH)
    pl.semaphore_signal(barrier, inc=1, device_id={"groups": og}, device_id_type=MESH)

    own_ad = pltpu.make_async_copy(adapter_hbm, ad.at[me], local.at[0])
    own_hist = pltpu.make_async_copy(hist_hbm, hist, local.at[1])
    own_wk = pltpu.make_async_copy(wk_hbm, wk, local.at[2])
    own_wv = pltpu.make_async_copy(wv_hbm, wv, local.at[3])
    small = [
        pltpu.make_async_copy(source, target, local.at[4 + place])
        for place, (source, target) in enumerate(
            ((routes_hbm, routes_ref), (iuser_hbm, iuser_ref), (cand_hbm, cand_ref), (huser_hbm, huser_ref))
        )
    ]
    for copy in (*small, own_hist, own_wk, own_wv, own_ad):
        copy.start()

    def feat_copy(s):
        return pltpu.make_async_copy(
            feats_hbm.at[:, pl.ds(pl.multiple_of(s * block, 128), block)], feats.at[s], feat_sem.at[s]
        )

    each(0, n, lambda s: feat_copy(s).start())
    pl.semaphore_wait(barrier, 2 + jnp.where(has_left, 1, 0) + jnp.where(has_right, 1, 0))

    def to_right(src, k, ref):
        return remote(
            ref, ad.at[src, share(g, r, k)], right_send.at[src * sub + k], z_recv.at[src * sub + k], {"hist": me + 1}
        )

    def to_left(src, k, ref):
        return remote(
            ref, ad.at[src, share(g, r, k)], left_send.at[src * sub + k], z_recv.at[src * sub + k], {"hist": me - 1}
        )

    def piece(src, a, b, k):
        return ad.at[src, share(a, b, k)]

    for k in range(sub):

        @pl.when(me < n - 1)
        def _():
            to_right(me, k, adapter_hbm.at[share(g, r, k)]).start()

        @pl.when(me > 0)
        def _():
            to_left(me, k, adapter_hbm.at[share(g, r, k)]).start()

    for copy in small:
        copy.wait()
    route_row = routes_ref[...].astype(F32)
    user_row = iuser_ref[...].astype(F32)

    def hot(row, count):
        shape = (count, row.shape[1])
        return jnp.where(iota(shape, 0).astype(F32) == row, 1.0, 0.0)

    owner_hot = hot(route_row, owners)
    user_hot = hot(user_row, USERS).astype(BF16)
    counts = lax.dot_general(owner_hot.astype(BF16), user_hot, NT, preferred_element_type=F32)
    meta[0:owners, 0:USERS] = counts
    meta[owners : owners + 1, 0:items] = user_row
    meta[owners + 1 : owners + 2, 0:items] = route_row
    meta_copy = remote(meta, meta_par, pair_send.at[0], pair_recv.at[0], {"rep": orep})
    meta_copy.start()

    cand_hot_t = hot(cand_ref[...].astype(F32), items)
    cand_hot = cand_hot_t.T.astype(BF16)
    cand_user = jnp.dot(
        jnp.broadcast_to(user_row, (8, items)).astype(BF16), cand_hot_t.astype(BF16), preferred_element_type=F32
    )
    event_row = huser_ref[...].astype(F32)
    event_hot = hot(event_row, USERS).astype(BF16)
    mine = jnp.where(iota((owners, events), 0) == me, 1.0, 0.0)
    event_counts = lax.dot_general(mine.astype(BF16), event_hot, NT, preferred_element_type=F32)

    meta_copy.wait_recv()
    summed = counts + event_counts + meta_par[0:owners, 0:USERS]
    tab_all[me, 0:n, 0:USERS] = summed[0:n]
    tab_all[me, n : n + 1, 0:cands] = cand_user[0:1]

    def t_copy(to):
        return remote(tab_all.at[me], tab_all.at[me], t_send.at[to], t_recv.at[me], {"hist": to})

    def hop(src, a, b, k, sends, recvs, where):
        ref = piece(src, a, b, k)
        return remote(ref, ref, sends.at[src * sub + k], recvs.at[src * sub + k], where)

    def spread(src, k):
        hop(src, g, r, k, y_send, y_recv, {"groups": og}).start()
        hop(src, g, r, k, p_send, p_recv, {"rep": orep}).start()

    def z_arrive(s):
        for k in range(sub):

            @pl.when(me >= s)
            def _():
                src = me - s
                ref = piece(src, g, r, k)
                to_right(src, k, ref).wait_recv()

                @pl.when(me < n - 1)
                def _():
                    to_right(src, k, ref).start()

                spread(src, k)

            @pl.when(me + s < n)
            def _():
                src = me + s
                ref = piece(src, g, r, k)
                to_left(src, k, ref).wait_recv()

                @pl.when(me > 0)
                def _():
                    to_left(src, k, ref).start()

                spread(src, k)

    def y_pass(src):
        for k in range(sub):
            hop(src, og, r, k, y_send, y_recv, {"groups": og}).wait_recv()
            hop(src, og, r, k, pp_send, pp_recv, {"rep": orep}).start()

    def y_arrive(s):
        @pl.when(me >= s)
        def _():
            y_pass(me - s)

        @pl.when(me + s < n)
        def _():
            y_pass(me + s)

    def project():
        own_hist.wait()
        own_wk.wait()
        own_wv.wait()
        step_rows = min(events, 512)
        for start in range(0, events, step_rows):
            part = hist[start : start + step_rows, :]
            k_all[start : start + step_rows, :] = jnp.dot(part, wk[...], preferred_element_type=F32).astype(BF16)
            v_all[start : start + step_rows, :] = jnp.dot(part, wv[...], preferred_element_type=F32).astype(BF16)

    def own_block():
        each(0, n, lambda s: feat_copy(s).wait())
        own_ad.wait()
        acc[...] = jnp.dot(feats[me], ad[me], preferred_element_type=F32)

    z_arrive(1)
    project()
    z_arrive(2)
    y_arrive(1)
    own_block()
    each(3, n, lambda s: (z_arrive(s), y_arrive(s - 1)))

    each(1, n, lambda d: t_copy(peer(n - d)).start())
    y_arrive(n - 1)

    def third(d):
        src = peer(d)
        for k in range(sub):
            hop(src, g, orep, k, p_send, p_recv, {"rep": orep}).wait_recv()
            hop(src, og, orep, k, pp_send, pp_recv, {"rep": orep}).wait_recv()
        acc[...] += jnp.dot(feats[src], ad[src], preferred_element_type=F32)

    each(1, n, third)

    embedded = acc[...].astype(BF16)
    own_q = jnp.dot(cand_hot, embedded, preferred_element_type=F32)
    q_all[me] = own_q.astype(BF16)

    def q_copy(to):
        return remote(q_all.at[me], q_all.at[me], q_send.at[to], q_recv.at[me], {"hist": to})

    each(1, n, lambda d: q_copy(peer(n - d)).start())
    k_all[events : events + items, :] = embedded
    v_all[events : events + items, :] = embedded
    emb_copy = remote(
        k_all.at[pl.ds(events, items)],
        k_all.at[pl.ds(events + items, items)],
        pair_send.at[1],
        pair_recv.at[1],
        {"rep": orep},
    )
    emb_copy.start()

    each(1, n, lambda d: remote(
        tab_all.at[peer(d)], tab_all.at[peer(d)], t_send.at[peer(d)], t_recv.at[peer(d)], {"hist": peer(d)}
    ).wait_recv())
    table = lax.fori_loop(
        0, n, lambda s, t: t + tab_all[s, 0:owners, 0:USERS], jnp.zeros((owners, USERS), F32)
    )
    table = jnp.where(iota((owners, USERS), 0) < n, table, 0.0)
    high = jnp.floor(table * (1.0 / 256.0))
    split = jnp.concatenate([high, table - 256.0 * high], axis=0).astype(BF16)

    def scale_of(users_hot, owners_hot):
        both = jnp.dot(split, users_hot, preferred_element_type=F32)
        found = 256.0 * both[0:owners] + both[owners:]
        return 1.0 / jnp.maximum(jnp.sum(found * owners_hot, axis=0, keepdims=True), 1.0)

    par_user = meta_par[owners : owners + 1, 0:items]
    par_route = meta_par[owners + 1 : owners + 2, 0:items]
    ent_user[:, 0:events] = jnp.broadcast_to(event_row, (8, events))
    ent_user[:, events : events + items] = jnp.broadcast_to(user_row, (8, items))
    ent_user[:, events + items :] = jnp.broadcast_to(par_user, (8, items))
    ent_scale[:, 0:events] = jnp.broadcast_to(scale_of(event_hot, mine), (8, events))
    ent_scale[:, events : events + items] = jnp.broadcast_to(scale_of(user_hot, owner_hot), (8, items))
    ent_scale[:, events + items :] = jnp.broadcast_to(
        scale_of(hot(par_user, USERS).astype(BF16), hot(par_route, owners)), (8, items)
    )

    head_of = iota((1, cols), 1) // HS
    eye = iota((cands, cands), 0) == iota((cands, cands), 1)
    width = math_block(entries)

    def user_column(p):
        row = tab_all[p, n : n + 1, 0:cands]
        return jnp.sum(jnp.where(eye, row, 0.0), axis=1, keepdims=True)

    def q_wait(p):
        remote(q_all.at[p], q_all.at[p], q_send.at[p], q_recv.at[p], {"hist": p}).wait_recv()

    def o_copy(to):
        return remote(part_out.at[to], part_in.at[me], o_send.at[to], o_recv.at[me], {"hist": to})

    def chunk(p, opening):
        if not opening:
            q_wait(p)
        q = q_all[p] * jnp.asarray(0.5 * HS**-0.5, BF16)
        ucol = user_column(p)
        count = cands
        stacked = jnp.concatenate([jnp.where(head_of == h, q, jnp.zeros_like(q)) for h in range(heads)], axis=0)
        for start in range(0, entries, width):
            if opening and start + width > events + items and start <= events + items:
                emb_copy.wait_recv()
                v_all[events + items :, :] = k_all[events + items :, :]
            half = lax.dot_general(stacked, k_all[start : start + width, :], NT, preferred_element_type=F32)
            scale = jnp.where(
                ucol == ent_user[0:1, start : start + width], ent_scale[0:1, start : start + width], 0.0
            )
            weight = (half + half * jnp.tanh(half)).reshape(heads, count, width) * scale[None]
            w_scr[:, start : start + width] = weight.reshape(heads * count, width).astype(BF16)
        mixed = jnp.dot(w_scr[...], v_all[...], preferred_element_type=F32)
        total = mixed[0:count]
        for h in range(1, heads):
            total = jnp.where(head_of == h, mixed[h * count : (h + 1) * count], total)
        if opening:
            own_part[...] = total
        else:
            part_out[p] = total.astype(BF16)
            o_copy(p).start()

    chunk(me, True)
    each(1, n, lambda d: chunk(peer(d), False))

    def collect(d):
        src = peer(d)
        remote(part_out.at[src], part_in.at[src], o_send.at[src], o_recv.at[src], {"hist": src}).wait_recv()
        own_part[...] += part_in[src].astype(F32)

    each(1, n, collect)
    gate = own_q * (0.5 + 0.5 * jnp.tanh(0.5 * own_q))
    out_ref[...] = (gate * own_part[...]).astype(BF16)

    def drain(d):
        p = peer(d)
        for k in range(sub):
            hop(p, g, r, k, y_send, y_recv, {"groups": og}).wait_send()
            hop(p, g, r, k, p_send, p_recv, {"rep": orep}).wait_send()
            hop(p, og, r, k, pp_send, pp_recv, {"rep": orep}).wait_send()
        t_copy(p).wait_send()
        q_copy(p).wait_send()
        o_copy(p).wait_send()

    each(1, n, drain)

    def drain_right(s):
        @pl.when((me >= s) & (me < n - 1))
        def _():
            for k in range(sub):
                to_right(me - s, k, piece(me - s, g, r, k)).wait_send()

    def drain_left(s):
        @pl.when((me + s < n) & (me > 0))
        def _():
            for k in range(sub):
                to_left(me + s, k, piece(me + s, g, r, k)).wait_send()

    each(0, n, lambda s: (drain_right(s), drain_left(s)))
    meta_copy.wait_send()
    emb_copy.wait_send()


def math_block(entries):
    return 256 if entries % 256 == 0 else 128


def body(item_feats, adapter, hist_emb, key_weight, value_weight, routes, cand_index, item_user, hist_user):
    n = lax.axis_size("hist")
    items, depth = item_feats.shape
    block, cols = adapter.shape
    events, dim = hist_emb.shape
    cands = cand_index.shape[0]
    heads = cols // HS
    owners = up(n, 8)
    sub = pieces(block)
    wide = up(max(USERS, items, cands), 128)
    entries = events + 2 * items
    hbm = pl.BlockSpec(memory_space=pltpu.HBM)
    vmem = pl.BlockSpec(memory_space=pltpu.VMEM)
    dma = pltpu.SemaphoreType.DMA
    return pl.pallas_call(
        functools.partial(kernel, n),
        out_shape=jax.ShapeDtypeStruct((cands, cols), BF16),
        in_specs=[hbm] * 9,
        out_specs=vmem,
        scratch_shapes=[
            pltpu.VMEM((1, items), jnp.int32),
            pltpu.VMEM((1, cands), jnp.int32),
            pltpu.VMEM((1, items), jnp.int32),
            pltpu.VMEM((1, events), jnp.int32),
            pltpu.VMEM((n, items, block), BF16),
            pltpu.VMEM((n, block, cols), BF16),
            pltpu.VMEM((events, dim), BF16),
            pltpu.VMEM((dim, cols), BF16),
            pltpu.VMEM((dim, cols), BF16),
            pltpu.VMEM((entries, cols), BF16),
            pltpu.VMEM((entries, cols), BF16),
            pltpu.VMEM((items, cols), F32),
            pltpu.VMEM((n, cands, cols), BF16),
            pltpu.VMEM((n, cands, cols), BF16),
            pltpu.VMEM((n, cands, cols), BF16),
            pltpu.VMEM((cands, cols), F32),
            pltpu.VMEM((owners + 8, wide), F32),
            pltpu.VMEM((owners + 8, wide), F32),
            pltpu.VMEM((n, up(n + 1, 8), wide), F32),
            pltpu.VMEM((8, entries), F32),
            pltpu.VMEM((8, entries), F32),
            pltpu.VMEM((heads * cands, entries), BF16),
            dma((8,)),
            dma((n,)),
        ]
        + [dma((n * sub,))] * 9
        + [dma((n,))] * 6
        + [dma((2,)), dma((2,))],
        compiler_params=pltpu.CompilerParams(
            collective_id=0, has_side_effects=True
        ),
    )(
        item_feats,
        adapter,
        hist_emb,
        key_weight,
        value_weight,
        routes.reshape(1, items),
        cand_index.reshape(1, cands),
        item_user.reshape(1, items),
        hist_user.reshape(1, events),
    )


def solution(mesh):
    placed = (
        P(("groups", "hist", "rep"), None),
        P("hist", "head"),
        P(("groups", "hist"), None),
        P(None, "head"),
        P(None, "head"),
        P(("groups", "hist", "rep"), None),
        P(("groups", "hist", "rep")),
        P(("groups", "hist", "rep")),
        P(("groups", "hist")),
    )
    return jax.shard_map(
        body,
        mesh=mesh,
        in_specs=placed,
        out_specs=P(("groups", "hist", "rep"), "head"),
        check_vma=False,
    )
```
